32 devices in a mesh: tm: 8 (over y, x, core), space: 4 (over z).
Axes of the slice: x: 2, y: 2, z: 4, core: 2. Of those that a mesh axis runs over, the one named last changes fastest.
Arguments:
- node_fields: float32 [8, 5, 32, 128, 128], P('tm', None, 'space'), may hold values from -6 to 6
- region_label: int32 [32, 128, 128], P('space'), may hold values from 0 to 3
- sheet_shift: int32 [8, 128], P('tm'), may hold values from 0 to 1
- diffusivity: float32 [4], replicated, may hold values from 0.02 to 0.15
Outputs:
- updated_nodes: float32 [8, 5, 32, 128, 128], P('tm', None, 'space')
The draws below stay inside these ranges and needn't reach their ends.
All inputs are finite; a program needn't handle non-finite values.
Results may differ from the reference program's by a relative error of at most 0.00002.
Values sent between devices are 32-bit elements; how exact they have to be, the bound alone decides.
A program may use at most 64 MiB of HBM per device.

```python
import math
import jax
import jax.numpy as jnp
import numpy as np
from jax import lax

NX = 128
NY = 128
NODES = 5
REGIONS = 4
FINE_SWEEPS = 2
SLICES = 8
NZ = 32


def touch_ends(values, key, low, largest):
    dims = values.shape
    spot = [jax.random.randint(jax.random.fold_in(key, axis), (), 0, dims[axis]) for axis in range(len(dims))]
    values = values.at[tuple(spot)].set(low)
    longest = dims.index(max(dims))
    spot[longest] = (spot[longest] + 1) % dims[longest]
    return values.at[tuple(spot)].set(largest)


def level_of(rng, dims, cuts, low, top_value):
    gain, own = 1.0, jax.random.fold_in(rng, 6)
    for axis_at, blocks in cuts:
        steps = jnp.exp(jax.random.uniform(jax.random.fold_in(own, axis_at), (blocks,), jnp.float32, low / len(cuts), top_value / len(cuts)))
        gain = gain * jnp.repeat(steps, dims[axis_at] // blocks).reshape([-1 if axis == axis_at else 1 for axis in range(len(dims))])
    return gain


def gaussian(own_key, dims, scale, bound, shards=(), dtype=jnp.bfloat16):
    drawn = jax.random.normal(own_key, dims, jnp.float32) * scale
    if len(shards) > 0:
        drawn = level_of(own_key, dims, shards, -0.22, 0.18) * drawn
    return jnp.clip(drawn, min=-bound, max=bound).astype(dtype)


def setup_inputs(seed: int = 0) -> dict:
    arg_keys = jax.random.split(jax.random.key(seed), 5)
    node_fields = gaussian(arg_keys[0], (SLICES, NODES, NZ, NX, NY), 1.0, 6.0, ((0, 8), (2, 4)), jnp.float32)
    region_label = touch_ends(jax.random.randint(arg_keys[1], (NZ, NX, NY), 0, REGIONS), jax.random.fold_in(arg_keys[1], 1), 0, REGIONS - 1).astype(jnp.int32)
    sheet_shift = touch_ends(jax.random.randint(arg_keys[2], (SLICES, NY), 0, 2), jax.random.fold_in(arg_keys[2], 1), 0, 1).astype(jnp.int32)
    diffusivity = jnp.clip(jnp.exp(jax.random.uniform(arg_keys[3], (REGIONS,), jnp.float32, math.log(0.02), math.log(0.15))), 0.02, 0.15)
    return dict(node_fields=node_fields, region_label=region_label, sheet_shift=sheet_shift, diffusivity=diffusivity)


slice_length = 1.0

def node_tables():
    radius = math.sqrt(3.0 / 7.0)
    points = [0.0, (1.0 - radius) / 2.0, 0.5, (1.0 + radius) / 2.0, 1.0]
    integrals = np.zeros((4, 5))
    for column in range(5):
        coeffs = [1.0]
        divisor = 1.0
        for other in range(5):
            if other != column:
                anchor = points[other]
                product = [0.0] * (len(coeffs) + 1)
                for degree in range(len(coeffs)):
                    product[degree + 1] = product[degree + 1] + coeffs[degree]
                    product[degree] = product[degree] - anchor * coeffs[degree]
                coeffs = product
                divisor = divisor * (points[column] - anchor)
        for row in range(4):
            bottom = points[row]
            summit = points[row + 1]
            amount = 0.0
            for degree in range(len(coeffs)):
                amount = amount + coeffs[degree] / (degree + 1) * (summit ** (degree + 1) - bottom ** (degree + 1))
            integrals[row, column] = amount / divisor
    return (np.array(points), integrals)

def combine(coefficients, stack):
    total = float(coefficients[0]) * stack[0]
    for index in range(1, len(coefficients)):
        total = total + float(coefficients[index]) * stack[index]
    return total

def lookup(labels, table):
    result = jnp.zeros(labels.shape, jnp.float32)
    for region in range(table.shape[0]):
        result = result + jnp.where(labels == region, table[region], 0.0)
    return result

def restrict(field):
    shape = field.shape
    blocks = field.reshape(shape[:-3] + (shape[-3] // 4, 4, shape[-2] // 2, 2, shape[-1]))
    return lax.optimization_barrier(jnp.mean(blocks, axis=(-4, -2)))

def prolong(coarse):
    return jnp.repeat(jnp.repeat(coarse, 4, axis=-3), 2, axis=-2)

def pad_rows(field):
    return jnp.pad(field, [(0, 0)] * (field.ndim - 3) + [(1, 1), (0, 0), (0, 0)])

def neighbours(padded):
    center = padded[..., 1:-1, :, :]
    vertical = padded[..., 2:, :, :] + padded[..., :-2, :, :]
    across = jnp.roll(center, 1, -2) + jnp.roll(center, -1, -2)
    sideways = jnp.pad(center, [(0, 0)] * (center.ndim - 1) + [(1, 1)])
    lateral = sideways[..., 2:] + sideways[..., :-2]
    return (center, vertical, across, lateral)

def fine_rate(padded, kappa, advect):
    center, vertical, across, lateral = neighbours(padded)
    diffusion = kappa * (vertical + across + lateral - 6.0 * center)
    return diffusion - advect * (center - jnp.roll(center, 1, -2))

def coarse_rate(padded, kappa, advect):
    center, vertical, across, lateral = neighbours(padded)
    diffusion = kappa * ((vertical - 2.0 * center) / 16.0 + (across - 2.0 * center) / 4.0 + (lateral - 2.0 * center))
    return diffusion - 0.5 * advect * (center - jnp.roll(center, 1, -2))

def coarse_advance(initial, padded, kappa, advect, constant):
    return initial + slice_length * coarse_rate(padded, kappa, advect) + constant

def apply_correction(fields, delta_start, delta_end):
    times_table, integral_table = node_tables()
    pieces = []
    for node in range(NODES):
        weight = float(times_table[node])
        pieces.append(fields[node] + prolong((1.0 - weight) * delta_start + weight * delta_end))
    return jnp.stack(pieces)

def fine_sweeps(corrected, rates, kappa, advect, rims):
    times_table, integral_table = node_tables()
    old_values, old_rates = (corrected, rates)
    for sweep in range(FINE_SWEEPS):
        values = [old_values[0]]
        new_rates = [old_rates[0]]
        for node in range(NODES - 1):
            spacing = float(times_table[node + 1] - times_table[node]) * slice_length
            value = values[node] + spacing * (new_rates[node] - old_rates[node]) + slice_length * combine(integral_table[node], old_rates)
            values.append(value)
            if node < NODES - 2 or sweep < FINE_SWEEPS - 1:
                new_rates.append(fine_rate(rims(value[None]), kappa, advect)[0])
        old_values = jnp.stack(values)
        if sweep < FINE_SWEEPS - 1:
            old_rates = jnp.stack(new_rates)
    return old_values

def reference(node_fields, region_label, sheet_shift, diffusivity):
    times_table, integral_table = node_tables()
    weight_table = integral_table.sum(axis=0)
    kappa = lookup(region_label, diffusivity)
    kappa_coarse = restrict(kappa)
    advects = sheet_shift.astype(jnp.float32) / slice_length
    previous = jnp.concatenate([node_fields[0:1, 0], node_fields[:-1, NODES - 1]], 0)

    def prepare(inputs):
        fields, start, advect = inputs
        fields = jnp.concatenate([start[None], fields[1:]], 0)
        rates = fine_rate(pad_rows(fields), kappa, advect)
        coarse_start = restrict(start)
        moved = restrict(slice_length * combine(weight_table, rates))
        constant = moved - slice_length * coarse_rate(pad_rows(coarse_start), kappa_coarse, advect)
        return (coarse_start, constant)
    coarse_starts, constants = lax.map(prepare, (node_fields, previous, advects))

    def chain(carry, inputs):
        constant, advect = inputs
        ending = coarse_advance(carry, pad_rows(carry), kappa_coarse, advect, constant)
        return (ending, (carry, ending))
    finished, (begins, endings) = lax.scan(chain, coarse_starts[0], (constants, advects))

    def finish(inputs):
        fields, start, advect, begin, ending, coarse_start = inputs
        fields = jnp.concatenate([start[None], fields[1:]], 0)
        corrected = apply_correction(fields, begin - coarse_start, ending - restrict(fields[NODES - 1]))
        rates = fine_rate(pad_rows(corrected), kappa, advect)
        return fine_sweeps(corrected, rates, kappa, advect, pad_rows)
    return lax.map(finish, (node_fields, previous, advects, begins, endings, coarse_starts))
```

```python
import math

import jax
import jax.numpy as jnp
import numpy as np
from jax import lax
from jax.experimental import pallas as pl
from jax.experimental.pallas import tpu as pltpu
from jax.sharding import PartitionSpec as P

NODES = 5
FINE_SWEEPS = 2
BLOCK_Z = 4
BLOCK_X = 2
PAD = 8
MESH = pl.DeviceIdType.MESH

slice_length = 1.0


def node_tables():
    radius = math.sqrt(3.0 / 7.0)
    points = [0.0, (1.0 - radius) / 2.0, 0.5, (1.0 + radius) / 2.0, 1.0]
    integrals = np.zeros((4, 5))
    for column in range(5):
        coeffs = [1.0]
        divisor = 1.0
        for other in range(5):
            if other != column:
                anchor = points[other]
                product = [0.0] * (len(coeffs) + 1)
                for degree in range(len(coeffs)):
                    product[degree + 1] = product[degree + 1] + coeffs[degree]
                    product[degree] = product[degree] - anchor * coeffs[degree]
                coeffs = product
                divisor = divisor * (points[column] - anchor)
        for row in range(4):
            bottom = points[row]
            summit = points[row + 1]
            amount = 0.0
            for degree in range(len(coeffs)):
                amount = amount + coeffs[degree] / (degree + 1) * (
                    summit ** (degree + 1) - bottom ** (degree + 1)
                )
            integrals[row, column] = amount / divisor
    return (np.array(points), integrals)


TIMES, INTEGRALS = node_tables()
WEIGHTS = INTEGRALS.sum(axis=0)
STEPS = NODES - 1
EXCHANGES = 2 + FINE_SWEEPS * STEPS


class Transfer:
    def __init__(self, src, dst, send_sem, recv_sem, device, sends, receives):
        self.copy = pltpu.make_async_remote_copy(
            src_ref=src,
            dst_ref=dst,
            send_sem=send_sem,
            recv_sem=recv_sem,
            device_id=device,
            device_id_type=MESH,
        )
        self.sends, self.receives = sends, receives

    def start(self):
        pl.when(self.sends)(self.copy.start)

    def wait_recv(self):
        pl.when(self.receives)(self.copy.wait_recv)

    def wait_send(self):
        pl.when(self.sends)(self.copy.wait_send)


def kernel(
    fields, label, shift, table, out,
    kappa, kappa_c, start, moved, shift_next, below, pads, values, mids, spread, gain, lift, delta, ahead, fold,
    halo_send, halo_recv, time_send, time_recv,
):
    n, s = lax.axis_index("tm"), lax.axis_index("space")
    slices, slabs = lax.axis_size("tm"), lax.axis_size("space")
    depth, width, height = label.shape
    rows_c = width // BLOCK_X
    depth_c = depth // BLOCK_Z
    chunk = min(64, width)
    last = NODES - 1
    has_prev, has_next = n > 0, n < slices - 1
    has_low, has_high = s > 0, s < slabs - 1
    inner = pl.ds(PAD, width)

    barrier = pltpu.get_barrier_semaphore()
    met = jnp.int32(0)
    for dn in (-1, 0, 1):
        for ds in (-1, 0, 1):
            if dn == 0 and ds == 0:
                continue
            there = (n + dn >= 0) & (n + dn < slices) & (s + ds >= 0) & (s + ds < slabs)

            @pl.when(there)
            def _(dn=dn, ds=ds):
                pl.semaphore_signal(
                    barrier, inc=1, device_id={"tm": n + dn, "space": s + ds}, device_id_type=MESH
                )

            met = met + there.astype(jnp.int32)
    pl.semaphore_wait(barrier, met)

    shipped = []

    def send(transfer):
        transfer.start()
        shipped.append(transfer)
        return transfer

    def halo(index, low_src=None, high_src=None):
        buf = pads.at[index]
        low_src = buf.at[1, inner] if low_src is None else low_src
        high_src = buf.at[depth, inner] if high_src is None else high_src
        up = Transfer(
            high_src, buf.at[0, inner], halo_send.at[2 * index], halo_recv.at[2 * index],
            {"space": s + 1}, has_high, has_low,
        )
        down = Transfer(
            low_src, buf.at[depth + 1, inner], halo_send.at[2 * index + 1], halo_recv.at[2 * index + 1],
            {"space": s - 1}, has_low, has_high,
        )
        send(up)
        send(down)
        return (up, down)

    def arrive(pair):
        for transfer in pair:
            transfer.wait_recv()

    def time_hop(index, src, dst, ds=0):
        to = {"tm": n + 1} if ds == 0 else {"tm": n + 1, "space": s + ds}
        goes = has_next if ds == 0 else has_next & (s + ds >= 0) & (s + ds < slabs)
        comes = has_prev if ds == 0 else has_prev & (s - ds >= 0) & (s - ds < slabs)
        return Transfer(src, dst, time_send.at[index], time_recv.at[index], to, goes, comes)

    shift_hop = Transfer(
        shift, shift_next, time_send.at[0], time_recv.at[0], {"tm": n - 1}, has_prev, has_next
    )
    send(shift_hop)
    end_halo = halo(1, fields.at[last, 0], fields.at[last, depth - 1])
    start_hop = send(time_hop(1, fields.at[last], start))

    lane = lax.broadcasted_iota(jnp.int32, (chunk, height), 1)
    first_lane, last_lane = lane == 0, lane == height - 1
    lane_c = lax.broadcasted_iota(jnp.int32, (rows_c, height), 1)
    first_slice = (n == 0).astype(jnp.float32)

    def sideways(center, first, final):
        return jnp.where(final, 0.0, pltpu.roll(center, height - 1, 1)) + jnp.where(
            first, 0.0, pltpu.roll(center, 1, 1)
        )

    def rate(index, z, r, advect):
        center = pads[index, z + 1, pl.ds(PAD + r, chunk)]
        behind = pads[index, z + 1, pl.ds(PAD - 1 + r, chunk)]
        total = pads[index, z, pl.ds(PAD + r, chunk)] + pads[index, z + 2, pl.ds(PAD + r, chunk)]
        total = total + (behind + pads[index, z + 1, pl.ds(PAD + 1 + r, chunk)])
        total = total + sideways(center, first_lane, last_lane) - 6.0 * center
        return kappa[z, pl.ds(r, chunk)] * total - advect * (center - behind)

    def fill(index, z, r, value):
        pads[index, z + 1, pl.ds(PAD + r, chunk)] = value
        if r == 0:
            pads[index, z + 1, pl.ds(PAD + width, 1)] = value[:1]
        if r + chunk == width:
            pads[index, z + 1, pl.ds(PAD - 1, 1)] = value[chunk - 1 :]

    def each(lo, hi, body, place=lambda i: i):
        def turn(i, carry):
            z = place(i)
            for r in range(0, width, chunk):
                body(z, r)
            return carry

        lax.fori_loop(lo, hi, turn, 0)

    def edges(body):
        each(0, 2, body, lambda i: i * (depth - 1))

    def interior(body):
        each(1, depth - 1, body)

    def weigh(z, r):
        at = pl.ds(r, chunk)
        total = (first_slice * float(WEIGHTS[0])) * fields[0, z, at]
        for node in range(1, NODES):
            total = total + float(WEIGHTS[node]) * fields[node, z, at]
        fill(0, z, r, total)

    edges(weigh)
    weighted_halo = halo(0)
    interior(weigh)

    def prepare(z, r):
        at = pl.ds(r, chunk)
        fill(1, z, r, fields[last, z, at])
        labels = label[z, at]
        total = jnp.zeros((chunk, height), jnp.float32)
        for region in range(table.shape[0]):
            total = total + jnp.where(labels == region, table[region], 0.0)
        kappa[z, at] = total

    each(0, depth, prepare)

    for index in range(EXCHANGES):

        @pl.when(jnp.logical_not(has_low))
        def _(index=index):
            pads[index, 0, inner] = jnp.zeros((width, height), jnp.float32)

        @pl.when(jnp.logical_not(has_high))
        def _(index=index):
            pads[index, depth + 1, inner] = jnp.zeros((width, height), jnp.float32)

    def restrict(target, layer_of):
        def turn(zc, carry):
            for r in range(0, width, chunk):
                total = layer_of(BLOCK_Z * zc, r)
                for k in range(1, BLOCK_Z):
                    total = total + layer_of(BLOCK_Z * zc + k, r)
                fold[pl.ds(r, chunk)] = total
            total = fold[pl.ds(0, rows_c, stride=BLOCK_X)]
            for k in range(1, BLOCK_X):
                total = total + fold[pl.ds(k, rows_c, stride=BLOCK_X)]
            target[zc] = total * (1.0 / (BLOCK_Z * BLOCK_X))
            return carry

        lax.fori_loop(0, depth_c, turn, 0)

    advect = shift[...].astype(jnp.float32) / slice_length

    shift_hop.wait_recv()
    arrive(end_halo)
    advect_next = shift_next[...].astype(jnp.float32) / slice_length
    restrict(
        lift,
        lambda z, r: fields[last, z, pl.ds(r, chunk)]
        + (slice_length * float(WEIGHTS[0])) * rate(1, z, r, advect_next),
    )
    lift_hop = send(time_hop(2, lift, moved))

    restrict(kappa_c, lambda z, r: kappa[z, pl.ds(r, chunk)])
    arrive(weighted_halo)
    restrict(
        gain,
        lambda z, r: first_slice * fields[0, z, pl.ds(r, chunk)]
        - fields[last, z, pl.ds(r, chunk)]
        + slice_length * rate(0, z, r, advect),
    )

    @pl.when(jnp.logical_not(has_prev))
    def _():
        moved[...] = jnp.zeros_like(moved)
        delta[...] = jnp.zeros_like(delta)
        below[...] = jnp.zeros_like(below)

    @pl.when(has_prev & jnp.logical_not(has_low))
    def _():
        below[0] = jnp.zeros((rows_c, height), jnp.float32)

    @pl.when(has_prev & jnp.logical_not(has_high))
    def _():
        below[1] = jnp.zeros((rows_c, height), jnp.float32)

    body_hop = time_hop(3, ahead, delta)
    up_hop = time_hop(4, ahead.at[depth_c - 1], below.at[0], 1)
    down_hop = time_hop(5, ahead.at[0], below.at[1], -1)
    lift_hop.wait_recv()
    gain[...] = gain[...] + moved[...]
    body_hop.wait_recv()
    up_hop.wait_recv()
    down_hop.wait_recv()
    for zc in range(depth_c):
        center = delta[zc]
        under = below[0] if zc == 0 else delta[zc - 1]
        over = below[1] if zc == depth_c - 1 else delta[zc + 1]
        behind = pltpu.roll(center, 1, 0)
        across = behind + pltpu.roll(center, rows_c - 1, 0)
        lateral = sideways(center, lane_c == 0, lane_c == height - 1)
        spreading = kappa_c[zc] * (
            (under + over - 2.0 * center) * (1.0 / (BLOCK_Z * BLOCK_Z))
            + (across - 2.0 * center) * (1.0 / (BLOCK_X * BLOCK_X))
            + (lateral - 2.0 * center)
        )
        flow = (1.0 / BLOCK_X) * advect * (center - behind)
        ahead[zc] = center + slice_length * (spreading - flow) + gain[zc]
    send(body_hop)
    send(up_hop)
    send(down_hop)

    for zc in range(depth_c):
        for k in range(BLOCK_X):
            spread[0, zc, pl.ds(k, rows_c, stride=BLOCK_X)] = delta[zc]
            spread[1, zc, pl.ds(k, rows_c, stride=BLOCK_X)] = ahead[zc]

    start_hop.wait_recv()

    @pl.when(jnp.logical_not(has_prev))
    def _():
        def turn(z, carry):
            start[z] = fields[0, z]
            return carry

        lax.fori_loop(0, depth, turn, 0)

    def correct(z, r):
        at = pl.ds(r, chunk)
        zc = z // BLOCK_Z
        begin, ending = spread[0, zc, at], spread[1, zc, at]
        total = None
        for node in range(NODES):
            weight = float(TIMES[node])
            own = start[z, at] if node == 0 else fields[node, z, at]
            if node == 0:
                value = own + begin
                out[0, z, at] = value
            elif node == last:
                value = own + ending
            else:
                value = own + ((1.0 - weight) * begin + weight * ending)
            if node > 0:
                values[node - 1, z, at] = value
            term = (slice_length * float(INTEGRALS[0, node])) * value
            total = term if total is None else total + term
        fill(2, z, r, total)

    edges(correct)
    pair = halo(2)
    interior(correct)

    for sweep in range(FINE_SWEEPS):
        old = values if sweep == 0 else mids
        new = mids if sweep == 0 else None
        for step in range(STEPS):
            index = 2 + sweep * STEPS + step
            final = sweep == FINE_SWEEPS - 1
            more = not (final and step == STEPS - 1)

            def advance(z, r, index=index, step=step, old=old, new=new, final=final, more=more):
                at = pl.ds(r, chunk)
                if step == 0:
                    before = out[0, z, at]
                else:
                    before = out[step, z, at] if final else new[step - 1, z, at]
                value = before + rate(index, z, r, advect)
                if final:
                    out[step + 1, z, at] = value
                else:
                    new[step, z, at] = value
                if not more:
                    return
                if step < STEPS - 1:
                    gap = slice_length * float(TIMES[step + 2] - TIMES[step + 1])
                    total = gap * (value - old[step, z, at])
                    row, source, known = step + 1, old, {}
                else:
                    total, row, source, known = None, 0, new, {STEPS: value}
                for node in range(NODES):
                    if node == 0:
                        part = out[0, z, at]
                    else:
                        part = known[node] if node in known else source[node - 1, z, at]
                    term = (slice_length * float(INTEGRALS[row, node])) * part
                    total = term if total is None else total + term
                fill(index + 1, z, r, total)

            arrive(pair)
            edges(advance)
            if more:
                pair = halo(index + 1)
            interior(advance)

    for transfer in shipped:
        transfer.wait_send()


def shards(node_fields, region_label, sheet_shift, diffusivity):
    fields = node_fields[0]
    nodes, depth, width, height = fields.shape
    depth_c, rows_c = depth // BLOCK_Z, width // BLOCK_X
    f32 = jnp.float32
    fine = (depth, width, height)
    coarse = (depth_c, rows_c, height)
    vmem = pl.BlockSpec(memory_space=pltpu.VMEM)
    result = pl.pallas_call(
        kernel,
        out_shape=jax.ShapeDtypeStruct(fields.shape, f32),
        in_specs=[vmem, vmem, vmem, pl.BlockSpec(memory_space=pltpu.SMEM)],
        out_specs=vmem,
        scratch_shapes=[
            pltpu.VMEM(fine, f32),
            pltpu.VMEM(coarse, f32),
            pltpu.VMEM(fine, f32),
            pltpu.VMEM(coarse, f32),
            pltpu.VMEM(sheet_shift.shape, jnp.int32),
            pltpu.VMEM((2, rows_c, height), f32),
            pltpu.VMEM((EXCHANGES, depth + 2, width + 2 * PAD, height), f32),
            pltpu.VMEM((STEPS,) + fine, f32),
            pltpu.VMEM((STEPS,) + fine, f32),
            pltpu.VMEM((2, depth_c, width, height), f32),
            pltpu.VMEM(coarse, f32),
            pltpu.VMEM(coarse, f32),
            pltpu.VMEM(coarse, f32),
            pltpu.VMEM(coarse, f32),
            pltpu.VMEM((width, height), f32),
            pltpu.SemaphoreType.DMA((2 * EXCHANGES,)),
            pltpu.SemaphoreType.DMA((2 * EXCHANGES,)),
            pltpu.SemaphoreType.DMA((6,)),
            pltpu.SemaphoreType.DMA((6,)),
        ],
        compiler_params=pltpu.CompilerParams(
            collective_id=0, has_side_effects=True, vmem_limit_bytes=48 * 1024 * 1024
        ),
    )(fields, region_label, sheet_shift, diffusivity)
    return result[None]


def solution(mesh):
    in_specs = (P("tm", None, "space", None, None), P("space", None, None), P("tm", None), P())
    out_specs = P("tm", None, "space", None, None)
    return jax.shard_map(shards, mesh=mesh, in_specs=in_specs, out_specs=out_specs, check_vma=False)
```

```python
import math

import jax
import jax.numpy as jnp
import numpy as np
from jax import lax
from jax.experimental import pallas as pl
from jax.experimental.pallas import tpu as pltpu
from jax.sharding import PartitionSpec as P

NODES = 5
FINE_SWEEPS = 2
BLOCK_Z = 4
BLOCK_X = 2
PAD = 8
PIECES = 4
MESH = pl.DeviceIdType.MESH

slice_length = 1.0


def node_tables():
    radius = math.sqrt(3.0 / 7.0)
    points = [0.0, (1.0 - radius) / 2.0, 0.5, (1.0 + radius) / 2.0, 1.0]
    integrals = np.zeros((4, 5))
    for column in range(5):
        coeffs = [1.0]
        divisor = 1.0
        for other in range(5):
            if other != column:
                anchor = points[other]
                product = [0.0] * (len(coeffs) + 1)
                for degree in range(len(coeffs)):
                    product[degree + 1] = product[degree + 1] + coeffs[degree]
                    product[degree] = product[degree] - anchor * coeffs[degree]
                coeffs = product
                divisor = divisor * (points[column] - anchor)
        for row in range(4):
            bottom = points[row]
            summit = points[row + 1]
            amount = 0.0
            for degree in range(len(coeffs)):
                amount = amount + coeffs[degree] / (degree + 1) * (
                    summit ** (degree + 1) - bottom ** (degree + 1)
                )
            integrals[row, column] = amount / divisor
    return (np.array(points), integrals)


TIMES, INTEGRALS = node_tables()
WEIGHTS = INTEGRALS.sum(axis=0)
STEPS = NODES - 1
EXCHANGES = 2 + FINE_SWEEPS * STEPS


class Transfer:
    def __init__(self, src, dst, send_sem, recv_sem, device, sends, receives):
        self.copy = pltpu.make_async_remote_copy(
            src_ref=src,
            dst_ref=dst,
            send_sem=send_sem,
            recv_sem=recv_sem,
            device_id=device,
            device_id_type=MESH,
        )
        self.sends, self.receives = sends, receives

    def start(self):
        pl.when(self.sends)(self.copy.start)

    def wait_recv(self):
        pl.when(self.receives)(self.copy.wait_recv)

    def wait_send(self):
        pl.when(self.sends)(self.copy.wait_send)


def kernel(
    fields_in, label_in, shift_in, table_in, out, fields, label, shift, table,
    kappa, kappa_c, start, moved, shift_next, below, pads, values, mids, spread, gain, lift, delta, ahead, fold,
    halo_send, halo_recv, time_send, time_recv, load_sem,
):
    n, s = lax.axis_index("tm"), lax.axis_index("space")
    slices, slabs = lax.axis_size("tm"), lax.axis_size("space")
    depth, width, height = label.shape
    rows_c = width // BLOCK_X
    depth_c = depth // BLOCK_Z
    chunk = min(64, width)
    piece = width // PIECES
    last = NODES - 1
    has_prev, has_next = n > 0, n < slices - 1
    has_low, has_high = s > 0, s < slabs - 1
    inner = pl.ds(PAD, width)

    loads = [
        pltpu.make_async_copy(fields_in.at[node], fields.at[node], load_sem.at[node])
        for node in range(NODES)
    ]
    loads += [
        pltpu.make_async_copy(label_in, label, load_sem.at[NODES]),
        pltpu.make_async_copy(shift_in, shift, load_sem.at[NODES + 1]),
        pltpu.make_async_copy(table_in, table, load_sem.at[NODES + 2]),
    ]
    for load in loads:
        load.start()

    barrier = pltpu.get_barrier_semaphore()
    met = jnp.int32(0)
    for dn in (-1, 0, 1):
        for ds in (-1, 0, 1):
            if dn == 0 and ds == 0:
                continue
            there = (n + dn >= 0) & (n + dn < slices) & (s + ds >= 0) & (s + ds < slabs)

            @pl.when(there)
            def _(dn=dn, ds=ds):
                pl.semaphore_signal(
                    barrier, inc=1, device_id={"tm": n + dn, "space": s + ds}, device_id_type=MESH
                )

            met = met + there.astype(jnp.int32)
    pl.semaphore_wait(barrier, met)

    shipped = []

    def send(transfer):
        transfer.start()
        shipped.append(transfer)
        return transfer

    def halo(index, source=None):
        buf = pads.at[index]
        pieces = []
        for k in range(PIECES):
            rows = pl.ds(PAD + k * piece, piece)
            if source is None:
                low, high = buf.at[1, rows], buf.at[depth, rows]
            else:
                low, high = (source.at[z, pl.ds(k * piece, piece)] for z in (0, depth - 1))
            sem = 2 * (index * PIECES + k)
            up = Transfer(
                high, buf.at[0, rows], halo_send.at[sem], halo_recv.at[sem],
                {"space": s + 1}, has_high, has_low,
            )
            down = Transfer(
                low, buf.at[depth + 1, rows], halo_send.at[sem + 1], halo_recv.at[sem + 1],
                {"space": s - 1}, has_low, has_high,
            )
            pieces.append((down, up))
        return pieces

    def arrive(pieces):
        for down, up in pieces:
            down.wait_recv()
            up.wait_recv()

    def time_hop(index, src, dst, ds=0):
        to = {"tm": n + 1} if ds == 0 else {"tm": n + 1, "space": s + ds}
        goes = has_next if ds == 0 else has_next & (s + ds >= 0) & (s + ds < slabs)
        comes = has_prev if ds == 0 else has_prev & (s - ds >= 0) & (s - ds < slabs)
        return Transfer(src, dst, time_send.at[index], time_recv.at[index], to, goes, comes)

    shift_hop = Transfer(
        shift_in, shift_next, time_send.at[0], time_recv.at[0], {"tm": n - 1}, has_prev, has_next
    )
    send(shift_hop)
    end_halo = halo(1, fields_in.at[last])
    for down, up in end_halo:
        send(down)
        send(up)
    start_hop = send(time_hop(1, fields_in.at[last], start))

    first_slice = (n == 0).astype(jnp.float32)

    def sideways(center):
        lane = lax.broadcasted_iota(jnp.int32, center.shape, 1)
        return jnp.where(lane == height - 1, 0.0, pltpu.roll(center, height - 1, 1)) + jnp.where(
            lane == 0, 0.0, pltpu.roll(center, 1, 1)
        )

    def rate(index, z, r, advect, chunk=chunk):
        center = pads[index, z + 1, pl.ds(PAD + r, chunk)]
        behind = pads[index, z + 1, pl.ds(PAD - 1 + r, chunk)]
        total = pads[index, z, pl.ds(PAD + r, chunk)] + pads[index, z + 2, pl.ds(PAD + r, chunk)]
        total = total + (behind + pads[index, z + 1, pl.ds(PAD + 1 + r, chunk)])
        total = total + sideways(center) - 6.0 * center
        return kappa[z, pl.ds(r, chunk)] * total - advect * (center - behind)

    def fill(index, z, r, value):
        rows = value.shape[0]
        pads[index, z + 1, pl.ds(PAD + r, rows)] = value
        if r == 0:
            pads[index, z + 1, pl.ds(PAD + width, 1)] = value[:1]
        if r + rows == width:
            pads[index, z + 1, pl.ds(PAD - 1, 1)] = value[rows - 1 :]

    def each(lo, hi, body):
        def turn(z, carry):
            for r in range(0, width, chunk):
                body(z, r, chunk)
            return carry

        lax.fori_loop(lo, hi, turn, 0)

    def edges(body, needs=None, gives=None):
        for k in range(PIECES):
            for side, z in ((0, 0), (1, depth - 1)):
                if needs is not None:
                    needs[k][1 - side].wait_recv()
                body(z, k * piece, piece)
                if gives is not None:
                    send(gives[k][side])

    def interior(body):
        each(1, depth - 1, body)

    def weigh(z, r, chunk):
        at = pl.ds(r, chunk)
        total = (first_slice * float(WEIGHTS[0])) * fields[0, z, at]
        for node in range(1, NODES):
            total = total + float(WEIGHTS[node]) * fields[node, z, at]
        fill(0, z, r, total)

    for load in loads:
        load.wait()
    weighted_halo = halo(0)
    edges(weigh, None, weighted_halo)
    interior(weigh)

    def prepare(z, r, chunk):
        at = pl.ds(r, chunk)
        fill(1, z, r, fields[last, z, at])
        labels = label[z, at]
        total = jnp.zeros((chunk, height), jnp.float32)
        for region in range(table.shape[0]):
            total = total + jnp.where(labels == region, table[region], 0.0)
        kappa[z, at] = total

    each(0, depth, prepare)

    for index in range(EXCHANGES):

        @pl.when(jnp.logical_not(has_low))
        def _(index=index):
            pads[index, 0, inner] = jnp.zeros((width, height), jnp.float32)

        @pl.when(jnp.logical_not(has_high))
        def _(index=index):
            pads[index, depth + 1, inner] = jnp.zeros((width, height), jnp.float32)

    def restrict(target, layer_of):
        def turn(zc, carry):
            for r in range(0, width, chunk):
                total = layer_of(BLOCK_Z * zc, r)
                for k in range(1, BLOCK_Z):
                    total = total + layer_of(BLOCK_Z * zc + k, r)
                fold[pl.ds(r, chunk)] = total
            total = fold[pl.ds(0, rows_c, stride=BLOCK_X)]
            for k in range(1, BLOCK_X):
                total = total + fold[pl.ds(k, rows_c, stride=BLOCK_X)]
            target[zc] = total * (1.0 / (BLOCK_Z * BLOCK_X))
            return carry

        lax.fori_loop(0, depth_c, turn, 0)

    advect = shift[...].astype(jnp.float32) / slice_length

    shift_hop.wait_recv()
    arrive(end_halo)
    advect_next = shift_next[...].astype(jnp.float32) / slice_length
    restrict(
        lift,
        lambda z, r: fields[last, z, pl.ds(r, chunk)]
        + (slice_length * float(WEIGHTS[0])) * rate(1, z, r, advect_next),
    )
    lift_hop = send(time_hop(2, lift, moved))

    restrict(kappa_c, lambda z, r: kappa[z, pl.ds(r, chunk)])
    arrive(weighted_halo)
    restrict(
        gain,
        lambda z, r: first_slice * fields[0, z, pl.ds(r, chunk)]
        - fields[last, z, pl.ds(r, chunk)]
        + slice_length * rate(0, z, r, advect),
    )

    @pl.when(jnp.logical_not(has_prev))
    def _():
        moved[...] = jnp.zeros_like(moved)
        delta[...] = jnp.zeros_like(delta)
        below[...] = jnp.zeros_like(below)

    @pl.when(has_prev & jnp.logical_not(has_low))
    def _():
        below[0] = jnp.zeros((rows_c, height), jnp.float32)

    @pl.when(has_prev & jnp.logical_not(has_high))
    def _():
        below[1] = jnp.zeros((rows_c, height), jnp.float32)

    body_hop = time_hop(3, ahead, delta)
    up_hop = time_hop(4, ahead.at[depth_c - 1], below.at[0], 1)
    down_hop = time_hop(5, ahead.at[0], below.at[1], -1)
    lift_hop.wait_recv()
    gain[...] = gain[...] + moved[...]
    body_hop.wait_recv()
    up_hop.wait_recv()
    down_hop.wait_recv()
    for zc in range(depth_c):
        center = delta[zc]
        under = below[0] if zc == 0 else delta[zc - 1]
        over = below[1] if zc == depth_c - 1 else delta[zc + 1]
        behind = pltpu.roll(center, 1, 0)
        across = behind + pltpu.roll(center, rows_c - 1, 0)
        lateral = sideways(center)
        spreading = kappa_c[zc] * (
            (under + over - 2.0 * center) * (1.0 / (BLOCK_Z * BLOCK_Z))
            + (across - 2.0 * center) * (1.0 / (BLOCK_X * BLOCK_X))
            + (lateral - 2.0 * center)
        )
        flow = (1.0 / BLOCK_X) * advect * (center - behind)
        ahead[zc] = center + slice_length * (spreading - flow) + gain[zc]
    send(body_hop)
    send(up_hop)
    send(down_hop)

    for zc in range(depth_c):
        for k in range(BLOCK_X):
            spread[0, zc, pl.ds(k, rows_c, stride=BLOCK_X)] = delta[zc]
            spread[1, zc, pl.ds(k, rows_c, stride=BLOCK_X)] = ahead[zc]

    start_hop.wait_recv()

    @pl.when(jnp.logical_not(has_prev))
    def _():
        def turn(z, carry):
            start[z] = fields[0, z]
            return carry

        lax.fori_loop(0, depth, turn, 0)

    def correct(z, r, chunk):
        at = pl.ds(r, chunk)
        zc = z // BLOCK_Z
        begin, ending = spread[0, zc, at], spread[1, zc, at]
        total = None
        for node in range(NODES):
            weight = float(TIMES[node])
            own = start[z, at] if node == 0 else fields[node, z, at]
            if node == 0:
                value = own + begin
                out[0, z, at] = value
            elif node == last:
                value = own + ending
            else:
                value = own + ((1.0 - weight) * begin + weight * ending)
            if node > 0:
                values[node - 1, z, at] = value
            term = (slice_length * float(INTEGRALS[0, node])) * value
            total = term if total is None else total + term
        fill(2, z, r, total)

    pair = halo(2)
    edges(correct, None, pair)
    interior(correct)

    for sweep in range(FINE_SWEEPS):
        old = values if sweep == 0 else mids
        new = mids if sweep == 0 else None
        for step in range(STEPS):
            index = 2 + sweep * STEPS + step
            final = sweep == FINE_SWEEPS - 1
            more = not (final and step == STEPS - 1)

            def advance(z, r, chunk, index=index, step=step, old=old, new=new, final=final, more=more):
                at = pl.ds(r, chunk)
                if step == 0:
                    before = out[0, z, at]
                else:
                    before = out[step, z, at] if final else new[step - 1, z, at]
                value = before + rate(index, z, r, advect, chunk)
                if final:
                    out[step + 1, z, at] = value
                else:
                    new[step, z, at] = value
                if not more:
                    return
                if step < STEPS - 1:
                    gap = slice_length * float(TIMES[step + 2] - TIMES[step + 1])
                    total = gap * (value - old[step, z, at])
                    row, source, known = step + 1, old, {}
                else:
                    total, row, source, known = None, 0, new, {STEPS: value}
                for node in range(NODES):
                    if node == 0:
                        part = out[0, z, at]
                    else:
                        part = known[node] if node in known else source[node - 1, z, at]
                    term = (slice_length * float(INTEGRALS[row, node])) * part
                    total = term if total is None else total + term
                fill(index + 1, z, r, total)

            following = halo(index + 1) if more else None
            edges(advance, pair, following)
            interior(advance)
            pair = following

    for transfer in shipped:
        transfer.wait_send()


def shards(node_fields, region_label, sheet_shift, diffusivity):
    fields = node_fields[0]
    nodes, depth, width, height = fields.shape
    depth_c, rows_c = depth // BLOCK_Z, width // BLOCK_X
    f32 = jnp.float32
    fine = (depth, width, height)
    coarse = (depth_c, rows_c, height)
    vmem, hbm = (pl.BlockSpec(memory_space=space) for space in (pltpu.VMEM, pltpu.HBM))
    result = pl.pallas_call(
        kernel,
        out_shape=jax.ShapeDtypeStruct(fields.shape, f32),
        in_specs=[hbm] * 4,
        out_specs=vmem,
        scratch_shapes=[
            pltpu.VMEM(fields.shape, f32),
            pltpu.VMEM(fine, jnp.int32),
            pltpu.VMEM(sheet_shift.shape, jnp.int32),
            pltpu.SMEM(diffusivity.shape, f32),
            pltpu.VMEM(fine, f32),
            pltpu.VMEM(coarse, f32),
            pltpu.VMEM(fine, f32),
            pltpu.VMEM(coarse, f32),
            pltpu.VMEM(sheet_shift.shape, jnp.int32),
            pltpu.VMEM((2, rows_c, height), f32),
            pltpu.VMEM((EXCHANGES, depth + 2, width + 2 * PAD, height), f32),
            pltpu.VMEM((STEPS,) + fine, f32),
            pltpu.VMEM((STEPS,) + fine, f32),
            pltpu.VMEM((2, depth_c, width, height), f32),
            pltpu.VMEM(coarse, f32),
            pltpu.VMEM(coarse, f32),
            pltpu.VMEM(coarse, f32),
            pltpu.VMEM(coarse, f32),
            pltpu.VMEM((width, height), f32),
            pltpu.SemaphoreType.DMA((2 * EXCHANGES * PIECES,)),
            pltpu.SemaphoreType.DMA((2 * EXCHANGES * PIECES,)),
            pltpu.SemaphoreType.DMA((6,)),
            pltpu.SemaphoreType.DMA((6,)),
            pltpu.SemaphoreType.DMA((NODES + 3,)),
        ],
        compiler_params=pltpu.CompilerParams(
            collective_id=0, has_side_effects=True, vmem_limit_bytes=67043328
        ),
    )(fields, region_label, sheet_shift, diffusivity)
    return result[None]


def solution(mesh):
    in_specs = (P("tm", None, "space", None, None), P("space", None, None), P("tm", None), P())
    out_specs = P("tm", None, "space", None, None)
    return jax.shard_map(shards, mesh=mesh, in_specs=in_specs, out_specs=out_specs, check_vma=False)
```

```python
import math

import jax
import jax.numpy as jnp
import numpy as np
from jax import lax
from jax.experimental import pallas as pl
from jax.experimental.pallas import tpu as pltpu
from jax.sharding import PartitionSpec as P

NODES = 5
FINE_SWEEPS = 2
BLOCK_Z = 4
BLOCK_X = 2
PAD = 8
PIECES = 4
MESH = pl.DeviceIdType.MESH

slice_length = 1.0


def node_tables():
    radius = math.sqrt(3.0 / 7.0)
    points = [0.0, (1.0 - radius) / 2.0, 0.5, (1.0 + radius) / 2.0, 1.0]
    integrals = np.zeros((4, 5))
    for column in range(5):
        coeffs = [1.0]
        divisor = 1.0
        for other in range(5):
            if other != column:
                anchor = points[other]
                product = [0.0] * (len(coeffs) + 1)
                for degree in range(len(coeffs)):
                    product[degree + 1] = product[degree + 1] + coeffs[degree]
                    product[degree] = product[degree] - anchor * coeffs[degree]
                coeffs = product
                divisor = divisor * (points[column] - anchor)
        for row in range(4):
            bottom = points[row]
            summit = points[row + 1]
            amount = 0.0
            for degree in range(len(coeffs)):
                amount = amount + coeffs[degree] / (degree + 1) * (
                    summit ** (degree + 1) - bottom ** (degree + 1)
                )
            integrals[row, column] = amount / divisor
    return (np.array(points), integrals)


TIMES, INTEGRALS = node_tables()
WEIGHTS = INTEGRALS.sum(axis=0)
STEPS = NODES - 1
EXCHANGES = 2 + FINE_SWEEPS * STEPS


class Transfer:
    def __init__(self, src, dst, send_sem, recv_sem, device, sends, receives):
        self.copy = pltpu.make_async_remote_copy(
            src_ref=src,
            dst_ref=dst,
            send_sem=send_sem,
            recv_sem=recv_sem,
            device_id=device,
            device_id_type=MESH,
        )
        self.sends, self.receives = sends, receives

    def start(self):
        pl.when(self.sends)(self.copy.start)

    def wait_recv(self):
        pl.when(self.receives)(self.copy.wait_recv)

    def wait_send(self):
        pl.when(self.sends)(self.copy.wait_send)


def kernel(
    fields_in, label_in, shift_in, table_in, out, fields, label, shift, table,
    kappa, kappa_c, start, moved, shift_next, below, pads, values, mids, spread, gain, lift, delta, ahead, fold,
    halo_send, halo_recv, time_send, time_recv, load_sem,
):
    n, s = lax.axis_index("tm"), lax.axis_index("space")
    slices, slabs = lax.axis_size("tm"), lax.axis_size("space")
    depth, width, height = label.shape
    rows_c = width // BLOCK_X
    depth_c = depth // BLOCK_Z
    chunk = min(64, width)
    piece = width // PIECES
    last = NODES - 1
    has_prev, has_next = n > 0, n < slices - 1
    has_low, has_high = s > 0, s < slabs - 1
    inner = pl.ds(PAD, width)

    loads = [
        pltpu.make_async_copy(fields_in.at[node], fields.at[node], load_sem.at[node])
        for node in range(NODES)
    ]
    loads += [
        pltpu.make_async_copy(label_in, label, load_sem.at[NODES]),
        pltpu.make_async_copy(shift_in, shift, load_sem.at[NODES + 1]),
        pltpu.make_async_copy(table_in, table, load_sem.at[NODES + 2]),
    ]
    for load in loads:
        load.start()

    barrier = pltpu.get_barrier_semaphore()
    met = jnp.int32(0)
    for dn in (-1, 0, 1):
        for ds in (-1, 0, 1):
            if dn == 0 and ds == 0:
                continue
            there = (n + dn >= 0) & (n + dn < slices) & (s + ds >= 0) & (s + ds < slabs)

            @pl.when(there)
            def _(dn=dn, ds=ds):
                pl.semaphore_signal(
                    barrier, inc=1, device_id={"tm": n + dn, "space": s + ds}, device_id_type=MESH
                )

            met = met + there.astype(jnp.int32)
    pl.semaphore_wait(barrier, met)

    shipped = []

    def send(transfer):
        transfer.start()
        shipped.append(transfer)
        return transfer

    def halo(index, source=None):
        buf = pads.at[index]
        pieces = []
        for k in range(PIECES):
            rows = pl.ds(PAD + k * piece, piece)
            if source is None:
                low, high = buf.at[1, rows], buf.at[depth, rows]
            else:
                low, high = (source.at[z, pl.ds(k * piece, piece)] for z in (0, depth - 1))
            sem = 2 * (index * PIECES + k)
            up = Transfer(
                high, buf.at[0, rows], halo_send.at[sem], halo_recv.at[sem],
                {"space": s + 1}, has_high, has_low,
            )
            down = Transfer(
                low, buf.at[depth + 1, rows], halo_send.at[sem + 1], halo_recv.at[sem + 1],
                {"space": s - 1}, has_low, has_high,
            )
            pieces.append((down, up))
        return pieces

    def arrive(pieces):
        for down, up in pieces:
            down.wait_recv()
            up.wait_recv()

    def time_hop(index, src, dst, ds=0):
        to = {"tm": n + 1} if ds == 0 else {"tm": n + 1, "space": s + ds}
        goes = has_next if ds == 0 else has_next & (s + ds >= 0) & (s + ds < slabs)
        comes = has_prev if ds == 0 else has_prev & (s - ds >= 0) & (s - ds < slabs)
        return Transfer(src, dst, time_send.at[index], time_recv.at[index], to, goes, comes)

    shift_hop = Transfer(
        shift_in, shift_next, time_send.at[0], time_recv.at[0], {"tm": n - 1}, has_prev, has_next
    )
    send(shift_hop)
    end_halo = halo(1, fields_in.at[last])
    for down, up in end_halo:
        send(down)
        send(up)
    start_hop = send(time_hop(1, fields_in.at[last], start))

    first_slice = (n == 0).astype(jnp.float32)

    def sideways(center):
        lane = lax.broadcasted_iota(jnp.int32, center.shape, 1)
        return jnp.where(lane == height - 1, 0.0, pltpu.roll(center, height - 1, 1)) + jnp.where(
            lane == 0, 0.0, pltpu.roll(center, 1, 1)
        )

    def rate(index, z, r, advect, chunk=chunk):
        center = pads[index, z + 1, pl.ds(PAD + r, chunk)]
        behind = pads[index, z + 1, pl.ds(PAD - 1 + r, chunk)]
        total = pads[index, z, pl.ds(PAD + r, chunk)] + pads[index, z + 2, pl.ds(PAD + r, chunk)]
        total = total + (behind + pads[index, z + 1, pl.ds(PAD + 1 + r, chunk)])
        total = total + sideways(center) - 6.0 * center
        return kappa[z, pl.ds(r, chunk)] * total - advect * (center - behind)

    def fill(index, z, r, value):
        rows = value.shape[0]
        pads[index, z + 1, pl.ds(PAD + r, rows)] = value
        if r == 0:
            pads[index, z + 1, pl.ds(PAD + width, 1)] = value[:1]
        if r + rows == width:
            pads[index, z + 1, pl.ds(PAD - 1, 1)] = value[rows - 1 :]

    def each(lo, hi, body):
        def turn(z, carry):
            for r in range(0, width, chunk):
                body(z, r, chunk)
            return carry

        lax.fori_loop(lo, hi, turn, 0)

    def edges(body, needs=None, gives=None):
        for k in range(PIECES):
            if needs is not None:
                arrive(needs[k : k + 1])
            body(0, k * piece, piece)
            body(depth - 1, k * piece, piece)
            if gives is not None:
                send(gives[k][0])
                send(gives[k][1])

    def interior(body):
        each(1, depth - 1, body)

    def weigh(z, r, chunk):
        at = pl.ds(r, chunk)
        total = (first_slice * float(WEIGHTS[0])) * fields[0, z, at]
        for node in range(1, NODES):
            total = total + float(WEIGHTS[node]) * fields[node, z, at]
        fill(0, z, r, total)

    for load in loads:
        load.wait()
    weighted_halo = halo(0)
    edges(weigh, None, weighted_halo)
    interior(weigh)

    def prepare(z, r, chunk):
        at = pl.ds(r, chunk)
        fill(1, z, r, fields[last, z, at])
        labels = label[z, at]
        total = jnp.zeros((chunk, height), jnp.float32)
        for region in range(table.shape[0]):
            total = total + jnp.where(labels == region, table[region], 0.0)
        kappa[z, at] = total

    each(0, depth, prepare)

    for index in range(EXCHANGES):

        @pl.when(jnp.logical_not(has_low))
        def _(index=index):
            pads[index, 0, inner] = jnp.zeros((width, height), jnp.float32)

        @pl.when(jnp.logical_not(has_high))
        def _(index=index):
            pads[index, depth + 1, inner] = jnp.zeros((width, height), jnp.float32)

    def restrict(target, layer_of):
        def turn(zc, carry):
            for r in range(0, width, chunk):
                total = layer_of(BLOCK_Z * zc, r)
                for k in range(1, BLOCK_Z):
                    total = total + layer_of(BLOCK_Z * zc + k, r)
                fold[pl.ds(r, chunk)] = total
            total = fold[pl.ds(0, rows_c, stride=BLOCK_X)]
            for k in range(1, BLOCK_X):
                total = total + fold[pl.ds(k, rows_c, stride=BLOCK_X)]
            target[zc] = total * (1.0 / (BLOCK_Z * BLOCK_X))
            return carry

        lax.fori_loop(0, depth_c, turn, 0)

    advect = shift[...].astype(jnp.float32) / slice_length

    shift_hop.wait_recv()
    arrive(end_halo)
    advect_next = shift_next[...].astype(jnp.float32) / slice_length
    restrict(
        lift,
        lambda z, r: fields[last, z, pl.ds(r, chunk)]
        + (slice_length * float(WEIGHTS[0])) * rate(1, z, r, advect_next),
    )
    lift_hop = send(time_hop(2, lift, moved))

    restrict(kappa_c, lambda z, r: kappa[z, pl.ds(r, chunk)])
    arrive(weighted_halo)
    restrict(
        gain,
        lambda z, r: first_slice * fields[0, z, pl.ds(r, chunk)]
        - fields[last, z, pl.ds(r, chunk)]
        + slice_length * rate(0, z, r, advect),
    )

    @pl.when(jnp.logical_not(has_prev))
    def _():
        moved[...] = jnp.zeros_like(moved)
        delta[...] = jnp.zeros_like(delta)
        below[...] = jnp.zeros_like(below)

    @pl.when(has_prev & jnp.logical_not(has_low))
    def _():
        below[0] = jnp.zeros((rows_c, height), jnp.float32)

    @pl.when(has_prev & jnp.logical_not(has_high))
    def _():
        below[1] = jnp.zeros((rows_c, height), jnp.float32)

    body_hop = time_hop(3, ahead, delta)
    up_hop = time_hop(4, ahead.at[depth_c - 1], below.at[0], 1)
    down_hop = time_hop(5, ahead.at[0], below.at[1], -1)
    lift_hop.wait_recv()
    gain[...] = gain[...] + moved[...]
    body_hop.wait_recv()
    up_hop.wait_recv()
    down_hop.wait_recv()
    for zc in range(depth_c):
        center = delta[zc]
        under = below[0] if zc == 0 else delta[zc - 1]
        over = below[1] if zc == depth_c - 1 else delta[zc + 1]
        behind = pltpu.roll(center, 1, 0)
        across = behind + pltpu.roll(center, rows_c - 1, 0)
        lateral = sideways(center)
        spreading = kappa_c[zc] * (
            (under + over - 2.0 * center) * (1.0 / (BLOCK_Z * BLOCK_Z))
            + (across - 2.0 * center) * (1.0 / (BLOCK_X * BLOCK_X))
            + (lateral - 2.0 * center)
        )
        flow = (1.0 / BLOCK_X) * advect * (center - behind)
        ahead[zc] = center + slice_length * (spreading - flow) + gain[zc]
        if zc == 0:
            send(down_hop)
        if zc == depth_c - 1:
            send(up_hop)
    send(body_hop)

    for zc in range(depth_c):
        for k in range(BLOCK_X):
            spread[0, zc, pl.ds(k, rows_c, stride=BLOCK_X)] = delta[zc]
            spread[1, zc, pl.ds(k, rows_c, stride=BLOCK_X)] = ahead[zc]

    start_hop.wait_recv()

    @pl.when(jnp.logical_not(has_prev))
    def _():
        def turn(z, carry):
            start[z] = fields[0, z]
            return carry

        lax.fori_loop(0, depth, turn, 0)

    def correct(z, r, chunk):
        at = pl.ds(r, chunk)
        zc = z // BLOCK_Z
        begin, ending = spread[0, zc, at], spread[1, zc, at]
        total = None
        for node in range(NODES):
            weight = float(TIMES[node])
            own = start[z, at] if node == 0 else fields[node, z, at]
            if node == 0:
                value = own + begin
                out[0, z, at] = value
            elif node == last:
                value = own + ending
            else:
                value = own + ((1.0 - weight) * begin + weight * ending)
            if node > 0:
                values[node - 1, z, at] = value
            term = (slice_length * float(INTEGRALS[0, node])) * value
            total = term if total is None else total + term
        fill(2, z, r, total)

    pair = halo(2)
    edges(correct, None, pair)
    interior(correct)

    for sweep in range(FINE_SWEEPS):
        old = values if sweep == 0 else mids
        new = mids if sweep == 0 else None
        for step in range(STEPS):
            index = 2 + sweep * STEPS + step
            final = sweep == FINE_SWEEPS - 1
            more = not (final and step == STEPS - 1)

            def advance(z, r, chunk, index=index, step=step, old=old, new=new, final=final, more=more):
                at = pl.ds(r, chunk)
                if step == 0:
                    before = out[0, z, at]
                else:
                    before = out[step, z, at] if final else new[step - 1, z, at]
                value = before + rate(index, z, r, advect, chunk)
                if final:
                    out[step + 1, z, at] = value
                else:
                    new[step, z, at] = value
                if not more:
                    return
                if step < STEPS - 1:
                    gap = slice_length * float(TIMES[step + 2] - TIMES[step + 1])
                    total = gap * (value - old[step, z, at])
                    row, source, known = step + 1, old, {}
                else:
                    total, row, source, known = None, 0, new, {STEPS: value}
                for node in range(NODES):
                    if node == 0:
                        part = out[0, z, at]
                    else:
                        part = known[node] if node in known else source[node - 1, z, at]
                    term = (slice_length * float(INTEGRALS[row, node])) * part
                    total = term if total is None else total + term
                fill(index + 1, z, r, total)

            following = halo(index + 1) if more else None
            edges(advance, pair, following)
            interior(advance)
            pair = following

    groups = {}
    for transfer in shipped:
        groups.setdefault(id(transfer.sends), []).append(transfer)
    for group in groups.values():

        @pl.when(group[0].sends)
        def _(group=group):
            for transfer in group:
                transfer.copy.wait_send()


def shards(node_fields, region_label, sheet_shift, diffusivity):
    fields = node_fields[0]
    nodes, depth, width, height = fields.shape
    depth_c, rows_c = depth // BLOCK_Z, width // BLOCK_X
    f32 = jnp.float32
    fine = (depth, width, height)
    coarse = (depth_c, rows_c, height)
    vmem, hbm = (pl.BlockSpec(memory_space=space) for space in (pltpu.VMEM, pltpu.HBM))
    result = pl.pallas_call(
        kernel,
        out_shape=jax.ShapeDtypeStruct(fields.shape, f32),
        in_specs=[hbm] * 4,
        out_specs=vmem,
        scratch_shapes=[
            pltpu.VMEM(fields.shape, f32),
            pltpu.VMEM(fine, jnp.int32),
            pltpu.VMEM(sheet_shift.shape, jnp.int32),
            pltpu.SMEM(diffusivity.shape, f32),
            pltpu.VMEM(fine, f32),
            pltpu.VMEM(coarse, f32),
            pltpu.VMEM(fine, f32),
            pltpu.VMEM(coarse, f32),
            pltpu.VMEM(sheet_shift.shape, jnp.int32),
            pltpu.VMEM((2, rows_c, height), f32),
            pltpu.VMEM((EXCHANGES, depth + 2, width + 2 * PAD, height), f32),
            pltpu.VMEM((STEPS,) + fine, f32),
            pltpu.VMEM((STEPS,) + fine, f32),
            pltpu.VMEM((2, depth_c, width, height), f32),
            pltpu.VMEM(coarse, f32),
            pltpu.VMEM(coarse, f32),
            pltpu.VMEM(coarse, f32),
            pltpu.VMEM(coarse, f32),
            pltpu.VMEM((width, height), f32),
            pltpu.SemaphoreType.DMA((2 * EXCHANGES * PIECES,)),
            pltpu.SemaphoreType.DMA((2 * EXCHANGES * PIECES,)),
            pltpu.SemaphoreType.DMA((6,)),
            pltpu.SemaphoreType.DMA((6,)),
            pltpu.SemaphoreType.DMA((NODES + 3,)),
        ],
        compiler_params=pltpu.CompilerParams(
            collective_id=0, has_side_effects=True, vmem_limit_bytes=48 * 1024 * 1024
        ),
    )(*(pltpu.with_memory_space_constraint(x, pltpu.HBM) for x in (fields, region_label, sheet_shift, diffusivity)))
    return result[None]


def solution(mesh):
    in_specs = (P("tm", None, "space", None, None), P("space", None, None), P("tm", None), P())
    out_specs = P("tm", None, "space", None, None)
    return jax.shard_map(shards, mesh=mesh, in_specs=in_specs, out_specs=out_specs, check_vma=False)
```

```python
import math

import jax
import jax.numpy as jnp
import numpy as np
from jax import lax
from jax.experimental import pallas as pl
from jax.experimental.pallas import tpu as pltpu
from jax.sharding import PartitionSpec as P

NODES = 5
FINE_SWEEPS = 2
BLOCK_Z = 4
BLOCK_X = 2
PAD = 8
PIECES = 4
MESH = pl.DeviceIdType.MESH

slice_length = 1.0


def node_tables():
    radius = math.sqrt(3.0 / 7.0)
    points = [0.0, (1.0 - radius) / 2.0, 0.5, (1.0 + radius) / 2.0, 1.0]
    integrals = np.zeros((4, 5))
    for column in range(5):
        coeffs = [1.0]
        divisor = 1.0
        for other in range(5):
            if other != column:
                anchor = points[other]
                product = [0.0] * (len(coeffs) + 1)
                for degree in range(len(coeffs)):
                    product[degree + 1] = product[degree + 1] + coeffs[degree]
                    product[degree] = product[degree] - anchor * coeffs[degree]
                coeffs = product
                divisor = divisor * (points[column] - anchor)
        for row in range(4):
            bottom = points[row]
            summit = points[row + 1]
            amount = 0.0
            for degree in range(len(coeffs)):
                amount = amount + coeffs[degree] / (degree + 1) * (
                    summit ** (degree + 1) - bottom ** (degree + 1)
                )
            integrals[row, column] = amount / divisor
    return (np.array(points), integrals)


TIMES, INTEGRALS = node_tables()
WEIGHTS = INTEGRALS.sum(axis=0)
STEPS = NODES - 1
EXCHANGES = 2 + FINE_SWEEPS * STEPS


class Transfer:
    def __init__(self, src, dst, send_sem, recv_sem, device, sends, receives):
        self.copy = pltpu.make_async_remote_copy(
            src_ref=src,
            dst_ref=dst,
            send_sem=send_sem,
            recv_sem=recv_sem,
            device_id=device,
            device_id_type=MESH,
        )
        self.sends, self.receives = sends, receives

    def start(self):
        pl.when(self.sends)(self.copy.start)

    def wait_recv(self):
        pl.when(self.receives)(self.copy.wait_recv)

    def wait_send(self):
        pl.when(self.sends)(self.copy.wait_send)


def kernel(
    fields_in, label_in, shift_in, table_in, out, fields, label, shift, table,
    kappa, kappa_c, start, moved, shift_next, below, pads, values, mids, spread, gain, lift, delta, ahead, fold,
    halo_send, halo_recv, time_send, time_recv, load_sem,
):
    n, s = lax.axis_index("tm"), lax.axis_index("space")
    slices, slabs = lax.axis_size("tm"), lax.axis_size("space")
    depth, width, height = label.shape
    rows_c = width // BLOCK_X
    depth_c = depth // BLOCK_Z
    chunk = min(64, width)
    piece = width // PIECES
    last = NODES - 1
    has_prev, has_next = n > 0, n < slices - 1
    has_low, has_high = s > 0, s < slabs - 1
    inner = pl.ds(PAD, width)

    loads = [
        pltpu.make_async_copy(fields_in.at[node], fields.at[node], load_sem.at[node])
        for node in range(NODES)
    ]
    loads += [
        pltpu.make_async_copy(label_in, label, load_sem.at[NODES]),
        pltpu.make_async_copy(shift_in, shift, load_sem.at[NODES + 1]),
        pltpu.make_async_copy(table_in, table, load_sem.at[NODES + 2]),
    ]
    for load in loads:
        load.start()

    barrier = pltpu.get_barrier_semaphore()
    met = jnp.int32(0)
    for dn in (-1, 0, 1):
        for ds in (-1, 0, 1):
            if dn == 0 and ds == 0:
                continue
            there = (n + dn >= 0) & (n + dn < slices) & (s + ds >= 0) & (s + ds < slabs)

            @pl.when(there)
            def _(dn=dn, ds=ds):
                pl.semaphore_signal(
                    barrier, inc=1, device_id={"tm": n + dn, "space": s + ds}, device_id_type=MESH
                )

            met = met + there.astype(jnp.int32)
    pl.semaphore_wait(barrier, met)

    shipped = []

    def send(transfer):
        transfer.start()
        shipped.append(transfer)
        return transfer

    def halo(index, source=None):
        buf = pads.at[index]
        pieces = []
        for k in range(PIECES):
            rows = pl.ds(PAD + k * piece, piece)
            if source is None:
                low, high = buf.at[1, rows], buf.at[depth, rows]
            else:
                low, high = (source.at[z, pl.ds(k * piece, piece)] for z in (0, depth - 1))
            sem = 2 * (index * PIECES + k)
            up = Transfer(
                high, buf.at[0, rows], halo_send.at[sem], halo_recv.at[sem],
                {"space": s + 1}, has_high, has_low,
            )
            down = Transfer(
                low, buf.at[depth + 1, rows], halo_send.at[sem + 1], halo_recv.at[sem + 1],
                {"space": s - 1}, has_low, has_high,
            )
            pieces.append((down, up))
        return pieces

    def arrive(pieces):
        for down, up in pieces:
            down.wait_recv()
            up.wait_recv()

    def time_hop(index, src, dst, ds=0):
        to = {"tm": n + 1} if ds == 0 else {"tm": n + 1, "space": s + ds}
        goes = has_next if ds == 0 else has_next & (s + ds >= 0) & (s + ds < slabs)
        comes = has_prev if ds == 0 else has_prev & (s - ds >= 0) & (s - ds < slabs)
        return Transfer(src, dst, time_send.at[index], time_recv.at[index], to, goes, comes)

    shift_hop = Transfer(
        shift_in, shift_next, time_send.at[0], time_recv.at[0], {"tm": n - 1}, has_prev, has_next
    )
    send(shift_hop)
    end_halo = halo(1, fields_in.at[last])
    for down, up in end_halo:
        send(down)
        send(up)
    start_hop = send(time_hop(1, fields_in.at[last], start))

    first_slice = (n == 0).astype(jnp.float32)

    def sideways(center):
        lane = lax.broadcasted_iota(jnp.int32, center.shape, 1)
        return jnp.where(lane == height - 1, 0.0, pltpu.roll(center, height - 1, 1)) + jnp.where(
            lane == 0, 0.0, pltpu.roll(center, 1, 1)
        )

    def rate(index, z, r, advect, chunk=chunk):
        center = pads[index, z + 1, pl.ds(PAD + r, chunk)]
        behind = pads[index, z + 1, pl.ds(PAD - 1 + r, chunk)]
        total = pads[index, z, pl.ds(PAD + r, chunk)] + pads[index, z + 2, pl.ds(PAD + r, chunk)]
        total = total + (behind + pads[index, z + 1, pl.ds(PAD + 1 + r, chunk)])
        total = total + sideways(center) - 6.0 * center
        return kappa[z, pl.ds(r, chunk)] * total - advect * (center - behind)

    def fill(index, z, r, value):
        rows = value.shape[0]
        pads[index, z + 1, pl.ds(PAD + r, rows)] = value
        if r == 0:
            pads[index, z + 1, pl.ds(PAD + width, 1)] = value[:1]
        if r + rows == width:
            pads[index, z + 1, pl.ds(PAD - 1, 1)] = value[rows - 1 :]

    def each(lo, hi, body):
        def turn(z, carry):
            for r in range(0, width, chunk):
                body(z, r, chunk)
            return carry

        lax.fori_loop(lo, hi, turn, 0)

    def edges(body, needs=None, gives=None):
        for k in range(PIECES):
            if needs is not None:
                arrive(needs[k : k + 1])
            body(0, k * piece, piece)
            body(depth - 1, k * piece, piece)
            if gives is not None:
                send(gives[k][0])
                send(gives[k][1])

    def interior(body):
        each(1, depth - 1, body)

    def weigh(z, r, chunk):
        at = pl.ds(r, chunk)
        total = (first_slice * float(WEIGHTS[0])) * fields[0, z, at]
        for node in range(1, NODES):
            total = total + float(WEIGHTS[node]) * fields[node, z, at]
        fill(0, z, r, total)

    for load in loads:
        load.wait()
    weighted_halo = halo(0)
    edges(weigh, None, weighted_halo)
    interior(weigh)

    def prepare(z, r, chunk):
        at = pl.ds(r, chunk)
        fill(1, z, r, fields[last, z, at])
        labels = label[z, at]
        total = jnp.zeros((chunk, height), jnp.float32)
        for region in range(table.shape[0]):
            total = total + jnp.where(labels == region, table[region], 0.0)
        kappa[z, at] = total

    each(0, depth, prepare)

    for index in range(EXCHANGES):

        @pl.when(jnp.logical_not(has_low))
        def _(index=index):
            pads[index, 0, inner] = jnp.zeros((width, height), jnp.float32)

        @pl.when(jnp.logical_not(has_high))
        def _(index=index):
            pads[index, depth + 1, inner] = jnp.zeros((width, height), jnp.float32)

    def restrict(target, layer_of):
        def turn(zc, carry):
            for r in range(0, width, chunk):
                total = layer_of(BLOCK_Z * zc, r)
                for k in range(1, BLOCK_Z):
                    total = total + layer_of(BLOCK_Z * zc + k, r)
                fold[pl.ds(r, chunk)] = total
            total = fold[pl.ds(0, rows_c, stride=BLOCK_X)]
            for k in range(1, BLOCK_X):
                total = total + fold[pl.ds(k, rows_c, stride=BLOCK_X)]
            target[zc] = total * (1.0 / (BLOCK_Z * BLOCK_X))
            return carry

        lax.fori_loop(0, depth_c, turn, 0)

    advect = shift[...].astype(jnp.float32) / slice_length

    shift_hop.wait_recv()
    arrive(end_halo)
    advect_next = shift_next[...].astype(jnp.float32) / slice_length
    restrict(
        lift,
        lambda z, r: fields[last, z, pl.ds(r, chunk)]
        + (slice_length * float(WEIGHTS[0])) * rate(1, z, r, advect_next),
    )
    lift_hop = send(time_hop(2, lift, moved))

    restrict(kappa_c, lambda z, r: kappa[z, pl.ds(r, chunk)])
    arrive(weighted_halo)
    restrict(
        gain,
        lambda z, r: first_slice * fields[0, z, pl.ds(r, chunk)]
        - fields[last, z, pl.ds(r, chunk)]
        + slice_length * rate(0, z, r, advect),
    )

    @pl.when(jnp.logical_not(has_prev))
    def _():
        moved[...] = jnp.zeros_like(moved)
        delta[...] = jnp.zeros_like(delta)
        below[...] = jnp.zeros_like(below)

    @pl.when(has_prev & jnp.logical_not(has_low))
    def _():
        below[0] = jnp.zeros((rows_c, height), jnp.float32)

    @pl.when(has_prev & jnp.logical_not(has_high))
    def _():
        below[1] = jnp.zeros((rows_c, height), jnp.float32)

    body_hop = time_hop(3, ahead, delta)
    up_hop = time_hop(4, ahead.at[depth_c - 1], below.at[0], 1)
    down_hop = time_hop(5, ahead.at[0], below.at[1], -1)
    start_hop.wait_recv()

    def combine_start(z, r, chunk):
        at = pl.ds(r, chunk)
        total = (slice_length * float(INTEGRALS[0, 0])) * start[z, at]
        for node in range(1, NODES):
            total = total + (slice_length * float(INTEGRALS[0, node])) * fields[node, z, at]
        fill(2, z, r, total)

    pl.when(has_prev)(lambda: edges(combine_start))
    lift_hop.wait_recv()
    gain[...] = gain[...] + moved[...]
    body_hop.wait_recv()
    up_hop.wait_recv()
    down_hop.wait_recv()
    for zc in range(depth_c):
        center = delta[zc]
        under = below[0] if zc == 0 else delta[zc - 1]
        over = below[1] if zc == depth_c - 1 else delta[zc + 1]
        behind = pltpu.roll(center, 1, 0)
        across = behind + pltpu.roll(center, rows_c - 1, 0)
        lateral = sideways(center)
        spreading = kappa_c[zc] * (
            (under + over - 2.0 * center) * (1.0 / (BLOCK_Z * BLOCK_Z))
            + (across - 2.0 * center) * (1.0 / (BLOCK_X * BLOCK_X))
            + (lateral - 2.0 * center)
        )
        flow = (1.0 / BLOCK_X) * advect * (center - behind)
        ahead[zc] = center + slice_length * (spreading - flow) + gain[zc]
        if zc == 0:
            send(down_hop)
        if zc == depth_c - 1:
            send(up_hop)
    send(body_hop)

    for zc in range(depth_c):
        for k in range(BLOCK_X):
            spread[0, zc, pl.ds(k, rows_c, stride=BLOCK_X)] = delta[zc]
            spread[1, zc, pl.ds(k, rows_c, stride=BLOCK_X)] = ahead[zc]

    @pl.when(jnp.logical_not(has_prev))
    def _():
        def turn(z, carry):
            start[z] = fields[0, z]
            return carry

        lax.fori_loop(0, depth, turn, 0)
        edges(combine_start)

    late = slice_length * float((INTEGRALS[0] * TIMES).sum())
    early = slice_length * float(INTEGRALS[0].sum()) - late

    def correct_edge(z, r, chunk):
        at, zc = pl.ds(r, chunk), z // BLOCK_Z
        base = pads[2, z + 1, pl.ds(PAD + r, chunk)]
        fill(2, z, r, base + (early * spread[0, zc, at] + late * spread[1, zc, at]))

    def correct(z, r, chunk):
        at = pl.ds(r, chunk)
        zc = z // BLOCK_Z
        begin, ending = spread[0, zc, at], spread[1, zc, at]
        total = None
        for node in range(NODES):
            weight = float(TIMES[node])
            own = start[z, at] if node == 0 else fields[node, z, at]
            if node == 0:
                value = own + begin
                out[0, z, at] = value
            elif node == last:
                value = own + ending
            else:
                value = own + ((1.0 - weight) * begin + weight * ending)
            if node > 0:
                values[node - 1, z, at] = value
            term = (slice_length * float(INTEGRALS[0, node])) * value
            total = term if total is None else total + term
        if not isinstance(z, int):
            fill(2, z, r, total)

    pair = halo(2)
    edges(correct_edge, None, pair)
    edges(correct)
    interior(correct)

    for sweep in range(FINE_SWEEPS):
        old = values if sweep == 0 else mids
        new = mids if sweep == 0 else None
        for step in range(STEPS):
            index = 2 + sweep * STEPS + step
            final = sweep == FINE_SWEEPS - 1
            more = not (final and step == STEPS - 1)

            def advance(z, r, chunk, index=index, step=step, old=old, new=new, final=final, more=more):
                at = pl.ds(r, chunk)
                if step == 0:
                    before = out[0, z, at]
                else:
                    before = out[step, z, at] if final else new[step - 1, z, at]
                value = before + rate(index, z, r, advect, chunk)
                if final:
                    out[step + 1, z, at] = value
                else:
                    new[step, z, at] = value
                if not more:
                    return
                if step < STEPS - 1:
                    gap = slice_length * float(TIMES[step + 2] - TIMES[step + 1])
                    total = gap * (value - old[step, z, at])
                    row, source, known = step + 1, old, {}
                else:
                    total, row, source, known = None, 0, new, {STEPS: value}
                for node in range(NODES):
                    if node == 0:
                        part = out[0, z, at]
                    else:
                        part = known[node] if node in known else source[node - 1, z, at]
                    term = (slice_length * float(INTEGRALS[row, node])) * part
                    total = term if total is None else total + term
                fill(index + 1, z, r, total)

            following = halo(index + 1) if more else None
            edges(advance, pair, following)
            interior(advance)
            pair = following

    groups = {}
    for transfer in shipped:
        groups.setdefault(id(transfer.sends), []).append(transfer)
    for group in groups.values():

        @pl.when(group[0].sends)
        def _(group=group):
            for transfer in group:
                transfer.copy.wait_send()


def shards(node_fields, region_label, sheet_shift, diffusivity):
    fields = node_fields[0]
    nodes, depth, width, height = fields.shape
    depth_c, rows_c = depth // BLOCK_Z, width // BLOCK_X
    f32 = jnp.float32
    fine = (depth, width, height)
    coarse = (depth_c, rows_c, height)
    vmem, hbm = (pl.BlockSpec(memory_space=space) for space in (pltpu.VMEM, pltpu.HBM))
    result = pl.pallas_call(
        kernel,
        out_shape=jax.ShapeDtypeStruct(fields.shape, f32),
        in_specs=[hbm] * 4,
        out_specs=vmem,
        scratch_shapes=[
            pltpu.VMEM(fields.shape, f32),
            pltpu.VMEM(fine, jnp.int32),
            pltpu.VMEM(sheet_shift.shape, jnp.int32),
            pltpu.SMEM(diffusivity.shape, f32),
            pltpu.VMEM(fine, f32),
            pltpu.VMEM(coarse, f32),
            pltpu.VMEM(fine, f32),
            pltpu.VMEM(coarse, f32),
            pltpu.VMEM(sheet_shift.shape, jnp.int32),
            pltpu.VMEM((2, rows_c, height), f32),
            pltpu.VMEM((EXCHANGES, depth + 2, width + 2 * PAD, height), f32),
            pltpu.VMEM((STEPS,) + fine, f32),
            pltpu.VMEM((STEPS,) + fine, f32),
            pltpu.VMEM((2, depth_c, width, height), f32),
            pltpu.VMEM(coarse, f32),
            pltpu.VMEM(coarse, f32),
            pltpu.VMEM(coarse, f32),
            pltpu.VMEM(coarse, f32),
            pltpu.VMEM((width, height), f32),
            pltpu.SemaphoreType.DMA((2 * EXCHANGES * PIECES,)),
            pltpu.SemaphoreType.DMA((2 * EXCHANGES * PIECES,)),
            pltpu.SemaphoreType.DMA((6,)),
            pltpu.SemaphoreType.DMA((6,)),
            pltpu.SemaphoreType.DMA((NODES + 3,)),
        ],
        compiler_params=pltpu.CompilerParams(
            collective_id=0, has_side_effects=True, vmem_limit_bytes=48 * 1024 * 1024
        ),
    )(*(pltpu.with_memory_space_constraint(x, pltpu.HBM) for x in (fields, region_label, sheet_shift, diffusivity)))
    return result[None]


def solution(mesh):
    in_specs = (P("tm", None, "space", None, None), P("space", None, None), P("tm", None), P())
    out_specs = P("tm", None, "space", None, None)
    return jax.shard_map(shards, mesh=mesh, in_specs=in_specs, out_specs=out_specs, check_vma=False)
```
